512 devices in a mesh: row: 8 (over y), col: 64 (over z, x, core).
Axes of the slice: x: 4, y: 8, z: 8, core: 2. Of those that a mesh axis runs over, the one named last changes fastest.
Arguments:
- ppmi: bfloat16 [4096, 128256], P('row', 'col'), may hold values from -12000 to 12000
- basis: bfloat16 [256, 128256], P(None, 'col'), may hold values from -10 to 10
Outputs:
- left_basis: bfloat16 [256, 4096], P(None, 'row')
- right_basis: bfloat16 [256, 128256], P(None, 'col')
The draws below stay inside these ranges and needn't reach their ends.
All inputs are finite; a program needn't handle non-finite values.
Results may differ from the reference program's by a relative error of at most 0.0045.
Values may be sent and summed in bfloat16 or wider, within the bound.
A program may use at most 128 MiB of HBM per device.

```python
import math
import jax
import jax.numpy as jnp
from jax import lax

K = 256
C_DEV = 2004
ITERS = 1
ROWS = 4096
VOCAB = 128256
N_ROW = 8


def draw_ppmi(key, part):
    key_rows, key_cols, key_cells = jax.random.split(jax.random.fold_in(key, 11), 3)
    row_scale = jnp.exp(jax.random.uniform(key_rows, (ROWS, 1), jnp.float32, 0.0, math.log(10.0)))
    col_scale = jnp.exp(jax.random.uniform(key_cols, (1, VOCAB), jnp.float32, 0.0, math.log(10.0)))
    cells = jnp.clip(jax.random.normal(key_cells, (ROWS, VOCAB), jnp.float32), -4.0, 4.0)
    heavy_count = (C_DEV + N_ROW - 1) // N_ROW
    heavy_factor = math.sqrt(VOCAB / heavy_count)
    positions = jnp.arange(VOCAB, dtype=jnp.int32).reshape(1, VOCAB)
    boost = jnp.where(positions < heavy_count, jnp.float32(heavy_factor), jnp.float32(1.0))
    return (row_scale * col_scale * boost * cells).astype(jnp.bfloat16)


def draw_basis(key, part):
    key_own, key_common = jax.random.split(jax.random.fold_in(key, 23), 2)
    own = jnp.clip(jax.random.normal(key_own, (K, VOCAB), jnp.float32), -4.0, 4.0)
    common = jnp.clip(jax.random.normal(key_common, (1, VOCAB), jnp.float32), -4.0, 4.0)
    return (own + common).astype(jnp.bfloat16)


def setup_inputs(seed: int = 0) -> dict:
    key_list = jax.random.split(jax.random.key(seed), 3)
    return {
        "ppmi": draw_ppmi(jax.random.fold_in(key_list[2], 71), 0),
        "basis": draw_basis(jax.random.fold_in(key_list[2], 71), 0),
    }


def orthonormal(block, count):
    gram = jnp.dot(block, block.T, precision=lax.Precision.HIGHEST) / count
    lower = jnp.linalg.cholesky(gram)
    solved = lax.linalg.triangular_solve(lower, block, left_side=True, lower=True)
    return solved.astype(jnp.bfloat16)

def reference(ppmi, basis):
    basis_now = basis
    left = None
    for turn in range(ITERS):
        y_full = lax.dot_general(basis_now.astype(jnp.float32), ppmi.astype(jnp.float32), (((1,), (1,)), ((), ())), preferred_element_type=jnp.float32)
        left = orthonormal(y_full, ROWS)
        z_full = jnp.dot(left.astype(jnp.float32), ppmi.astype(jnp.float32), preferred_element_type=jnp.float32)
        basis_now = orthonormal(z_full, VOCAB)
    return (left, basis_now)
```

```python
import functools

import jax
import jax.numpy as jnp
from jax import lax
from jax.experimental import pallas as pl
from jax.experimental.pallas import tpu as pltpu
from jax.sharding import Mesh
from jax.sharding import PartitionSpec as P

F32 = jnp.float32
BF16 = jnp.bfloat16
MESH = pl.DeviceIdType.MESH
NY, NZ, NX, NK = 8, 8, 4, 2
SIZES = {"row": NY, "z": NZ, "x": NX, "k": NK}
VMEM = pl.BlockSpec(memory_space=pltpu.VMEM)
LIMIT = 56 << 20


def peer(axis, step):
    return lax.rem(lax.axis_index(axis) + (step + SIZES[axis]), SIZES[axis])


def greet(axes):
    barrier = pltpu.get_barrier_semaphore()
    count = 0
    for axis in axes:
        for step in range(1, SIZES[axis]):
            pl.semaphore_signal(barrier, inc=1, device_id={axis: peer(axis, step)}, device_id_type=MESH)
            count += 1
    return lambda: pl.semaphore_wait(barrier, count)


class Exchange:
    def __init__(self, axis, source, target, send, recv):
        self.copies = []
        for step in range(1, SIZES[axis]):
            to = peer(axis, step)
            self.copies.append(
                pltpu.make_async_remote_copy(
                    src_ref=source(to),
                    dst_ref=target(step),
                    send_sem=send.at[step - 1],
                    recv_sem=recv.at[step - 1],
                    device_id={axis: to},
                    device_id_type=MESH,
                )
            )
        for copy in self.copies:
            copy.start()

    def arrived(self):
        for copy in self.copies:
            copy.wait_recv()

    def sent(self):
        for copy in self.copies:
            copy.wait_send()


def part(index, size):
    return pl.ds(pl.multiple_of(index * size, size), size)


def tile_of(ref, index, width):
    return ref.at[..., part(index // 2, 8), part(lax.rem(index, 2), width)]


def dot(a, b, dims, precision=None):
    return lax.dot_general(a, b, (dims, ((), ())), precision=precision, preferred_element_type=F32)


def y_kernel(b_ref, p_ref, y_ref, away, home, from_k, from_x, strip, from_z, tile, sends, recvs):
    z, x, k = (lax.axis_index(a) for a in ("z", "x", "k"))
    wait_barrier = greet(("z", "x", "k"))
    away[...] = dot(b_ref[part(1 - k, 128), :], p_ref[...], ((1,), (1,)))
    wait_barrier()
    ex_k = Exchange("k", lambda to: away, lambda step: from_k, sends.at[0], recvs.at[0])
    own = dot(b_ref[part(k, 128), :], p_ref[...], ((1,), (1,)))
    ex_k.arrived()
    home[...] = own + from_k[...]
    ex_x = Exchange("x", lambda to: home.at[part(to, 32)], lambda step: from_x.at[step - 1], sends.at[1], recvs.at[1])
    ex_x.arrived()
    strip[...] = home[part(x, 32), :] + from_x[0] + from_x[1] + from_x[2]
    ex_z = Exchange("z", lambda to: tile_of(strip, to, 256), lambda step: from_z.at[step - 1], sends.at[2], recvs.at[2])
    ex_z.arrived()
    total = strip[part(z // 2, 8), part(lax.rem(z, 2), 256)]
    for step in range(NZ - 1):
        total += from_z[step]
    tile[...] = total
    half = y_ref.at[part(k, 128)]
    rows = half.at[part(x, 32)]
    tile_of(rows, z, 256)[...] = total
    ag_z = Exchange("z", lambda to: tile, lambda step: tile_of(rows, z, 256), sends.at[3], recvs.at[3])
    ag_z.arrived()
    ag_x = Exchange("x", lambda to: rows, lambda step: rows, sends.at[4], recvs.at[4])
    ag_x.arrived()
    ag_k = Exchange("k", lambda to: half, lambda step: half, sends.at[5], recvs.at[5])
    ag_k.arrived()
    for ex in (ex_k, ex_x, ex_z, ag_z, ag_x, ag_k):
        ex.sent()


def hop(axis, step, source, target, send, recv):
    copy = pltpu.make_async_remote_copy(
        src_ref=source,
        dst_ref=target,
        send_sem=send,
        recv_sem=recv,
        device_id={axis: peer(axis, step)},
        device_id_type=MESH,
    )
    copy.start()
    return copy


def w_kernel(rows_total, cols_total, y_ref, p_ref, g_ref, w_ref, parts, ring, gram, gram1, from_k, home, from_x, strip, from_z,
             tile, from_y, piece, rs_send, rs_recv, ag_send, ag_recv, sends, recvs):
    row, z, x, k = (lax.axis_index(a) for a in ("row", "z", "x", "k"))
    cols = p_ref.shape[1]
    wait_barrier = greet(("row", "z", "x", "k"))
    y = y_ref[...]
    high = y.astype(BF16)
    low = (y - high.astype(F32)).astype(BF16)
    for chunk in range(NY):
        width = min(256, cols - 256 * chunk)
        block = p_ref[:, 256 * chunk : 256 * chunk + width]
        value = dot(high, block, ((1,), (0,))) + dot(low, block, ((1,), (0,)))
        if width < 256:
            parts[chunk] = jnp.zeros((256, 256), F32)
        parts[chunk, :, :width] = value
    wait_barrier()
    waiting = []
    ways = (1, -1)
    sub = 2
    size = 128 // sub

    def lines(way, piece_no):
        return pl.ds((0 if way == 1 else 128) + piece_no * size, size)

    for step in range(NY - 1):
        for piece_no in range(sub):
            for w, way in enumerate(ways):
                at = lines(way, piece_no)
                if step:
                    flight[w, piece_no].wait_recv()
                    ring[step - 1, at, :] += parts[peer("row", -way * (step + 1)), at, :]
                    source = ring.at[step - 1, at]
                else:
                    source = parts.at[peer("row", -way), at]
                    flight = {} if (piece_no == 0 and w == 0) else flight
                copy = hop("row", way, source, ring.at[step, at], rs_send.at[step, w, piece_no], rs_recv.at[step, w, piece_no])
                waiting.append(copy)
                flight[w, piece_no] = copy
    gram1[...] = dot(y, y, ((1,), (1,)), lax.Precision.HIGHEST) / rows_total
    for piece_no in range(sub):
        for w, way in enumerate(ways):
            at = lines(way, piece_no)
            flight[w, piece_no].wait_recv()
            w_ref[row, at, :] = ring[NY - 2, at, :] + parts[row, at, :]
    mine = w_ref[row]
    gram[...] = dot(mine, mine, ((1,), (1,)), lax.Precision.HIGHEST)
    passed = {}

    def pass_on(step):
        for w, way in enumerate(ways):
            at = pl.ds(128 * w, 128)
            if step:
                passed[w].wait_recv()
            if step < NY - 1:
                block = w_ref.at[peer("row", -way * step), at]
                passed[w] = hop("row", way, block, block, ag_send.at[step, w], ag_recv.at[step, w])
                waiting.append(passed[w])

    ex = [Exchange("k", lambda to: gram.at[part(to, 128)], lambda step: from_k, sends.at[0], recvs.at[0])]
    pass_on(0)
    ex[-1].arrived()
    home[...] = gram[part(k, 128), :] + from_k[...]
    ex.append(Exchange("x", lambda to: home.at[part(to, 32)], lambda step: from_x.at[step - 1], sends.at[1], recvs.at[1]))
    pass_on(1)
    ex[-1].arrived()
    strip[...] = home[part(x, 32), :] + from_x[0] + from_x[1] + from_x[2]
    ex.append(Exchange("z", lambda to: tile_of(strip, to, 128), lambda step: from_z.at[step - 1], sends.at[2], recvs.at[2]))
    pass_on(2)
    ex[-1].arrived()
    total = strip[part(z // 2, 8), part(lax.rem(z, 2), 128)]
    for step in range(NZ - 1):
        total += from_z[step]
    tile[0] = gram1[pl.ds(pl.multiple_of(128 * k + 32 * x + 8 * (z // 2), 8), 8), part(lax.rem(z, 2), 128)]
    tile[1] = total
    ex.append(Exchange("row", lambda to: tile, lambda step: from_y.at[step - 1], sends.at[3], recvs.at[3]))
    pass_on(3)
    ex[-1].arrived()
    whole = tile[...]
    for step in range(NY - 1):
        whole += from_y[step]
    whole = jnp.stack([whole[0], whole[1] / cols_total])
    piece[...] = whole
    half = g_ref.at[:, part(k, 128)]
    rows = half.at[:, part(x, 32)]
    tile_of(rows, z, 128)[...] = whole
    ex.append(Exchange("z", lambda to: piece, lambda step: tile_of(rows, z, 128), sends.at[4], recvs.at[4]))
    pass_on(4)
    ex[-1].arrived()
    ex.append(Exchange("x", lambda to: rows, lambda step: rows, sends.at[5], recvs.at[5]))
    pass_on(5)
    ex[-1].arrived()
    ex.append(Exchange("k", lambda to: half, lambda step: half, sends.at[6], recvs.at[6]))
    pass_on(6)
    ex[-1].arrived()
    pass_on(7)
    for e in ex:
        e.sent()
    for copy in waiting:
        copy.wait_send()


def in_three(value):
    high = value.astype(BF16).astype(F32)
    rest = value - high
    middle = rest.astype(BF16).astype(F32)
    return high, middle, rest - middle


def spread_pair(a, b):
    h, m, l = in_three(a)
    i, n, o = in_three(b)
    return jnp.concatenate([h, h, m, h, l, m], 0).astype(BF16), jnp.concatenate([i, n, i, o, i, n], 0).astype(BF16)


def eliminate(block, base, count):
    size = block.shape[1]
    lane = lax.broadcasted_iota(jnp.int32, (1, size), 1)
    line = lax.broadcasted_iota(jnp.int32, (count, 1), 0)
    for i in range(count):
        unit = lane == base + i
        root = lax.rsqrt(block[i : i + 1, base + i : base + i + 1])
        row = jnp.where(unit, root, block[i : i + 1, :] * root)
        weight = jnp.where(line > i, block[:, base + i : base + i + 1] * root, 0.0)
        cleared = jnp.where(unit & (line > i), 0.0, block)
        block = jnp.where(line == i, row, cleared - weight * row)
    return block


def finish_kernel(g_ref, y_ref, w_ref, left_ref, right_ref, work, inverse):
    size, count = 256, 32
    work[...] = g_ref[...]
    lane = lax.broadcasted_iota(jnp.int32, (1, size), 1)
    line = lax.broadcasted_iota(jnp.int32, (count, 1), 0)
    for base in range(0, size, count):
        below = base + count
        for q in range(2):
            block = eliminate(work[q, base:below, :], base, count)
            lower = lane <= line + base
            inverse[q, base:below, :] = jnp.where(lower, block, 0.0)
            if below < size:
                a, b = spread_pair(block, jnp.where(lower | (lane >= below), block, 0.0))
                change = dot(a, b, ((0,), (0,)))[below:]
                panel = (lane >= base) & (lane < below)
                work[q, below:, :] = jnp.where(panel, 0.0, work[q, below:, :]) - change
    left_ref[...] = dot(inverse[0], y_ref[...], ((1,), (0,)), lax.Precision.HIGHEST).astype(BF16)
    cols = right_ref.shape[1]
    for chunk in range(NY):
        width = min(256, cols - 256 * chunk)
        value = dot(inverse[1], w_ref[chunk], ((1,), (0,)), lax.Precision.HIGHEST).astype(BF16)
        right_ref[:, 256 * chunk : 256 * chunk + width] = value[:, :width]


def local(ppmi, basis):
    rows, cols = ppmi.shape
    rows_total, cols_total = rows * NY, cols * NZ * NX * NK
    dma = pltpu.SemaphoreType.DMA
    params = functools.partial(pltpu.CompilerParams, has_side_effects=True, vmem_limit_bytes=LIMIT)
    y = pl.pallas_call(
        y_kernel,
        out_shape=jax.ShapeDtypeStruct((256, 512), F32),
        in_specs=[VMEM] * 2,
        out_specs=VMEM,
        scratch_shapes=[
            pltpu.VMEM((128, 512), F32),
            pltpu.VMEM((128, 512), F32),
            pltpu.VMEM((128, 512), F32),
            pltpu.VMEM((3, 32, 512), F32),
            pltpu.VMEM((32, 512), F32),
            pltpu.VMEM((7, 8, 256), F32),
            pltpu.VMEM((8, 256), F32),
            dma((6, 7)),
            dma((6, 7)),
        ],
        compiler_params=params(collective_id=0),
    )(basis, ppmi)
    gram, w = pl.pallas_call(
        functools.partial(w_kernel, rows_total, cols_total),
        out_shape=[jax.ShapeDtypeStruct((2, 256, 256), F32), jax.ShapeDtypeStruct((8, 256, 256), F32)],
        in_specs=[VMEM] * 2,
        out_specs=[VMEM] * 2,
        scratch_shapes=[
            pltpu.VMEM((8, 256, 256), F32),
            pltpu.VMEM((7, 256, 256), F32),
            pltpu.VMEM((256, 256), F32),
            pltpu.VMEM((256, 256), F32),
            pltpu.VMEM((128, 256), F32),
            pltpu.VMEM((128, 256), F32),
            pltpu.VMEM((3, 32, 256), F32),
            pltpu.VMEM((32, 256), F32),
            pltpu.VMEM((7, 8, 128), F32),
            pltpu.VMEM((2, 8, 128), F32),
            pltpu.VMEM((7, 2, 8, 128), F32),
            pltpu.VMEM((2, 8, 128), F32),
            dma((7, 2, 2)),
            dma((7, 2, 2)),
            dma((7, 2)),
            dma((7, 2)),
            dma((7, 7)),
            dma((7, 7)),
        ],
        compiler_params=params(collective_id=1),
    )(y, ppmi)
    return pl.pallas_call(
        finish_kernel,
        out_shape=[jax.ShapeDtypeStruct((256, rows), BF16), jax.ShapeDtypeStruct((256, cols), BF16)],
        in_specs=[VMEM] * 3,
        out_specs=[VMEM] * 2,
        scratch_shapes=[pltpu.VMEM((2, 256, 256), F32), pltpu.VMEM((2, 256, 256), F32)],
        compiler_params=pltpu.CompilerParams(vmem_limit_bytes=LIMIT),
    )(gram, y, w)


def solution(mesh):
    split = Mesh(mesh.devices.reshape(NY, NZ, NX, NK), ("row", "z", "x", "k"))
    col = ("z", "x", "k")
    return jax.shard_map(
        local,
        mesh=split,
        in_specs=(P("row", col), P(None, col)),
        out_specs=(P(None, "row"), P(None, col)),
        check_vma=False,
    )
```

```python
import functools

import jax
import jax.numpy as jnp
from jax import lax
from jax.experimental import pallas as pl
from jax.experimental.pallas import tpu as pltpu
from jax.sharding import Mesh
from jax.sharding import PartitionSpec as P

F32 = jnp.float32
BF16 = jnp.bfloat16
MESH = pl.DeviceIdType.MESH
NY, NZ, NX, NK = 8, 8, 4, 2
SIZES = {"row": NY, "z": NZ, "x": NX, "k": NK}
VMEM = pl.BlockSpec(memory_space=pltpu.VMEM)
LIMIT = 56 << 20


def peer(axis, step):
    return lax.rem(lax.axis_index(axis) + (step + SIZES[axis]), SIZES[axis])


def greet(axes):
    barrier = pltpu.get_barrier_semaphore()
    count = 0
    for axis in axes:
        for step in range(1, SIZES[axis]):
            pl.semaphore_signal(barrier, inc=1, device_id={axis: peer(axis, step)}, device_id_type=MESH)
            count += 1
    return lambda: pl.semaphore_wait(barrier, count)


class Exchange:
    def __init__(self, axis, source, target, send, recv):
        self.copies = []
        for step in range(1, SIZES[axis]):
            to = peer(axis, step)
            self.copies.append(
                pltpu.make_async_remote_copy(
                    src_ref=source(to),
                    dst_ref=target(step),
                    send_sem=send.at[step - 1],
                    recv_sem=recv.at[step - 1],
                    device_id={axis: to},
                    device_id_type=MESH,
                )
            )
        for copy in self.copies:
            copy.start()

    def arrived(self):
        for copy in self.copies:
            copy.wait_recv()

    def sent(self):
        for copy in self.copies:
            copy.wait_send()


def part(index, size):
    return pl.ds(pl.multiple_of(index * size, size), size)


def tile_of(ref, index, width):
    return ref.at[..., part(index // 2, 8), part(lax.rem(index, 2), width)]


def dot(a, b, dims, precision=None):
    return lax.dot_general(a, b, (dims, ((), ())), precision=precision, preferred_element_type=F32)


def y_kernel(b_ref, p_ref, y_ref, away, home, from_k, from_x, strip, from_z, tile, sends, recvs):
    z, x, k = (lax.axis_index(a) for a in ("z", "x", "k"))
    wait_barrier = greet(("z", "x", "k"))
    away[...] = dot(b_ref[:, part(1 - k, 128)], p_ref[...], ((0,), (0,)))
    wait_barrier()
    ex_k = Exchange("k", lambda to: away, lambda step: from_k, sends.at[0], recvs.at[0])
    own = dot(b_ref[:, part(k, 128)], p_ref[...], ((0,), (0,)))
    ex_k.arrived()
    home[...] = own + from_k[...]
    ex_x = Exchange("x", lambda to: home.at[part(to, 32)], lambda step: from_x.at[step - 1], sends.at[1], recvs.at[1])
    ex_x.arrived()
    strip[...] = home[part(x, 32), :] + from_x[0] + from_x[1] + from_x[2]
    ex_z = Exchange("z", lambda to: tile_of(strip, to, 256), lambda step: from_z.at[step - 1], sends.at[2], recvs.at[2])
    ex_z.arrived()
    total = strip[part(z // 2, 8), part(lax.rem(z, 2), 256)]
    for step in range(NZ - 1):
        total += from_z[step]
    tile[...] = total
    half = y_ref.at[part(k, 128)]
    rows = half.at[part(x, 32)]
    tile_of(rows, z, 256)[...] = total
    ag_z = Exchange("z", lambda to: tile, lambda step: tile_of(rows, z, 256), sends.at[3], recvs.at[3])
    ag_z.arrived()
    ag_x = Exchange("x", lambda to: rows, lambda step: rows, sends.at[4], recvs.at[4])
    ag_x.arrived()
    ag_k = Exchange("k", lambda to: half, lambda step: half, sends.at[5], recvs.at[5])
    ag_k.arrived()
    for ex in (ex_k, ex_x, ex_z, ag_z, ag_x, ag_k):
        ex.sent()


def hop(axis, step, source, target, send, recv):
    copy = pltpu.make_async_remote_copy(
        src_ref=source,
        dst_ref=target,
        send_sem=send,
        recv_sem=recv,
        device_id={axis: peer(axis, step)},
        device_id_type=MESH,
    )
    copy.start()
    return copy


def w_kernel(rows_total, cols_total, y_ref, p_ref, g_ref, w_ref, parts, ring, gram, gram1, from_k, home, from_x, strip, from_z,
             tile, from_y, piece, rs_send, rs_recv, ag_send, ag_recv, sends, recvs):
    row, z, x, k = (lax.axis_index(a) for a in ("row", "z", "x", "k"))
    cols = p_ref.shape[0]
    wait_barrier = greet(("row", "z", "x", "k"))
    y = y_ref[...]
    high = y.astype(BF16)
    low = (y - high.astype(F32)).astype(BF16)
    for chunk in range(NY):
        width = min(256, cols - 256 * chunk)
        block = p_ref[256 * chunk : 256 * chunk + width, :]
        value = dot(block, high, ((1,), (1,))) + dot(block, low, ((1,), (1,)))
        if width < 256:
            parts[chunk, 128:, :] = jnp.zeros((128, 256), F32)
        parts[chunk, :width, :] = value
    wait_barrier()
    waiting = []
    ways = (1, -1)
    sub = 2
    size = 128 // sub

    def lines(way, piece_no):
        return pl.ds((0 if way == 1 else 128) + piece_no * size, size)

    for step in range(NY - 1):
        for piece_no in range(sub):
            for w, way in enumerate(ways):
                at = lines(way, piece_no)
                if step:
                    flight[w, piece_no].wait_recv()
                    ring[step - 1, at, :] += parts[peer("row", -way * (step + 1)), at, :]
                    source = ring.at[step - 1, at]
                else:
                    source = parts.at[peer("row", -way), at]
                    flight = {} if (piece_no == 0 and w == 0) else flight
                copy = hop("row", way, source, ring.at[step, at], rs_send.at[step, w, piece_no], rs_recv.at[step, w, piece_no])
                waiting.append(copy)
                flight[w, piece_no] = copy
    gram1[...] = dot(y, y, ((1,), (1,)), lax.Precision.HIGHEST) / rows_total
    for piece_no in range(sub):
        for w, way in enumerate(ways):
            at = lines(way, piece_no)
            flight[w, piece_no].wait_recv()
            w_ref[row, at, :] = ring[NY - 2, at, :] + parts[row, at, :]
    mine = w_ref[row]
    gram[...] = dot(mine, mine, ((0,), (0,)), lax.Precision.HIGHEST)
    passed = {}

    def pass_on(step):
        for w, way in enumerate(ways):
            at = pl.ds(128 * w, 128)
            if step:
                passed[w].wait_recv()
            if step < NY - 1:
                block = w_ref.at[peer("row", -way * step), at]
                passed[w] = hop("row", way, block, block, ag_send.at[step, w], ag_recv.at[step, w])
                waiting.append(passed[w])

    ex = [Exchange("k", lambda to: gram.at[part(to, 128)], lambda step: from_k, sends.at[0], recvs.at[0])]
    pass_on(0)
    ex[-1].arrived()
    home[...] = gram[part(k, 128), :] + from_k[...]
    ex.append(Exchange("x", lambda to: home.at[part(to, 32)], lambda step: from_x.at[step - 1], sends.at[1], recvs.at[1]))
    pass_on(1)
    ex[-1].arrived()
    strip[...] = home[part(x, 32), :] + from_x[0] + from_x[1] + from_x[2]
    ex.append(Exchange("z", lambda to: tile_of(strip, to, 128), lambda step: from_z.at[step - 1], sends.at[2], recvs.at[2]))
    pass_on(2)
    ex[-1].arrived()
    total = strip[part(z // 2, 8), part(lax.rem(z, 2), 128)]
    for step in range(NZ - 1):
        total += from_z[step]
    tile[0] = gram1[pl.ds(pl.multiple_of(128 * k + 32 * x + 8 * (z // 2), 8), 8), part(lax.rem(z, 2), 128)]
    tile[1] = total
    ex.append(Exchange("row", lambda to: tile, lambda step: from_y.at[step - 1], sends.at[3], recvs.at[3]))
    pass_on(3)
    ex[-1].arrived()
    whole = tile[...]
    for step in range(NY - 1):
        whole += from_y[step]
    whole = jnp.stack([whole[0], whole[1] / cols_total])
    piece[...] = whole
    half = g_ref.at[:, part(k, 128)]
    rows = half.at[:, part(x, 32)]
    tile_of(rows, z, 128)[...] = whole
    ex.append(Exchange("z", lambda to: piece, lambda step: tile_of(rows, z, 128), sends.at[4], recvs.at[4]))
    pass_on(4)
    ex[-1].arrived()
    ex.append(Exchange("x", lambda to: rows, lambda step: rows, sends.at[5], recvs.at[5]))
    pass_on(5)
    ex[-1].arrived()
    ex.append(Exchange("k", lambda to: half, lambda step: half, sends.at[6], recvs.at[6]))
    pass_on(6)
    ex[-1].arrived()
    pass_on(7)
    for e in ex:
        e.sent()
    for copy in waiting:
        copy.wait_send()


def in_three(value):
    high = value.astype(BF16).astype(F32)
    rest = value - high
    middle = rest.astype(BF16).astype(F32)
    return high, middle, rest - middle


def spread_pair(a, b):
    h, m, l = in_three(a)
    i, n, o = in_three(b)
    return jnp.concatenate([h, h, m, h, l, m], 0).astype(BF16), jnp.concatenate([i, n, i, o, i, n], 0).astype(BF16)


def spread(value):
    return jnp.broadcast_to(value, (8, 128))


def eliminate(block, base, count):
    lane = lax.broadcasted_iota(jnp.int32, (8, 128), 1)
    line = lax.broadcasted_iota(jnp.int32, (8, 128), 0)
    groups = count // 8
    tiles = [[block[8 * g : 8 * g + 8, 128 * h : 128 * h + 128] for g in range(groups)] for h in range(2)]
    for now in range(groups):
        side, first = divmod(base + 8 * now, 128)
        rows = [[spread(tiles[h][now][a : a + 1, :]) for h in range(2)] for a in range(8)]
        columns = [
            {g: spread(tiles[side][g][:, first + a : first + a + 1]) for g in range(now, groups)} for a in range(8)
        ]
        corner = {(i, k): spread(columns[k][now][i : i + 1, :]) for i in range(8) for k in range(i + 1)}
        factor, inverse = {}, {}
        for a in range(8):
            root = lax.rsqrt(corner[a, a])
            inverse[a, a] = root
            for i in range(a + 1, 8):
                factor[i, a] = corner[i, a] * root
            for i in range(a + 1, 8):
                for k in range(a + 1, i + 1):
                    corner[i, k] = corner[i, k] - factor[i, a] * factor[k, a]
            for k in range(a):
                total = factor[a, k] * inverse[k, k]
                for q in range(k + 1, a):
                    total = total + factor[a, q] * inverse[q, k]
                inverse[a, k] = -(total * root)
        done = []
        for a in range(8):
            pair = []
            for h in range(2):
                value = inverse[a, 0] * rows[0][h]
                for k in range(1, a + 1):
                    value = value + inverse[a, k] * rows[k][h]
                if h == side:
                    for k in range(8):
                        value = jnp.where(lane == first + k, inverse[a, k] if k <= a else 0.0, value)
                pair.append(value)
            done.append(pair)
        unit = (lane >= first) & (lane < first + 8)
        for g in range(now + 1, groups):
            weights = []
            for a in range(8):
                value = inverse[a, 0] * columns[0][g]
                for k in range(1, a + 1):
                    value = value + inverse[a, k] * columns[k][g]
                weights.append(value)
            for h in range(2):
                change = weights[0] * done[0][h]
                for a in range(1, 8):
                    change = change + weights[a] * done[a][h]
                old = jnp.where(unit, 0.0, tiles[h][g]) if h == side else tiles[h][g]
                tiles[h][g] = old - change
        for h in range(2):
            value = done[0][h]
            for a in range(1, 8):
                value = jnp.where(line == a, done[a][h], value)
            tiles[h][now] = value
    return jnp.concatenate([jnp.concatenate(tiles[h], 0) for h in range(2)], 1)


def finish_kernel(g_ref, y_ref, w_ref, left_ref, right_ref, work, inverse):
    size, count = 256, 16
    work[...] = g_ref[...]
    lane = lax.broadcasted_iota(jnp.int32, (1, size), 1)
    line = lax.broadcasted_iota(jnp.int32, (count, 1), 0)
    for base in range(0, size, count):
        below = base + count
        for q in range(2):
            block = eliminate(work[q, base:below, :], base, count)
            lower = lane <= line + base
            inverse[q, base:below, :] = jnp.where(lower, block, 0.0)
            if below < size:
                a, b = spread_pair(block, jnp.where(lower | (lane >= below), block, 0.0))
                change = dot(a, b, ((0,), (0,)))[below:]
                panel = (lane >= base) & (lane < below)
                work[q, below:, :] = jnp.where(panel, 0.0, work[q, below:, :]) - change
    left_ref[...] = dot(inverse[0], y_ref[...], ((1,), (0,)), lax.Precision.HIGHEST).astype(BF16)
    cols = right_ref.shape[0]
    for chunk in range(NY):
        width = min(256, cols - 256 * chunk)
        value = dot(w_ref[chunk, :width], inverse[1], ((1,), (1,)), lax.Precision.HIGHEST)
        right_ref[256 * chunk : 256 * chunk + width, :] = value.astype(BF16)


def local(ppmi, basis):
    rows, cols = ppmi.shape
    rows_total, cols_total = rows * NY, cols * NZ * NX * NK
    dma = pltpu.SemaphoreType.DMA
    params = functools.partial(pltpu.CompilerParams, has_side_effects=True, vmem_limit_bytes=LIMIT)
    y = pl.pallas_call(
        y_kernel,
        out_shape=jax.ShapeDtypeStruct((256, 512), F32),
        in_specs=[VMEM] * 2,
        out_specs=VMEM,
        scratch_shapes=[
            pltpu.VMEM((128, 512), F32),
            pltpu.VMEM((128, 512), F32),
            pltpu.VMEM((128, 512), F32),
            pltpu.VMEM((3, 32, 512), F32),
            pltpu.VMEM((32, 512), F32),
            pltpu.VMEM((7, 8, 256), F32),
            pltpu.VMEM((8, 256), F32),
            dma((6, 7)),
            dma((6, 7)),
        ],
        compiler_params=params(collective_id=0),
    )(basis.T, ppmi.T)
    gram, w = pl.pallas_call(
        functools.partial(w_kernel, rows_total, cols_total),
        out_shape=[jax.ShapeDtypeStruct((2, 256, 256), F32), jax.ShapeDtypeStruct((8, 256, 256), F32)],
        in_specs=[VMEM] * 2,
        out_specs=[VMEM] * 2,
        scratch_shapes=[
            pltpu.VMEM((8, 256, 256), F32),
            pltpu.VMEM((7, 256, 256), F32),
            pltpu.VMEM((256, 256), F32),
            pltpu.VMEM((256, 256), F32),
            pltpu.VMEM((128, 256), F32),
            pltpu.VMEM((128, 256), F32),
            pltpu.VMEM((3, 32, 256), F32),
            pltpu.VMEM((32, 256), F32),
            pltpu.VMEM((7, 8, 128), F32),
            pltpu.VMEM((2, 8, 128), F32),
            pltpu.VMEM((7, 2, 8, 128), F32),
            pltpu.VMEM((2, 8, 128), F32),
            dma((7, 2, 2)),
            dma((7, 2, 2)),
            dma((7, 2)),
            dma((7, 2)),
            dma((7, 7)),
            dma((7, 7)),
        ],
        compiler_params=params(collective_id=1),
    )(y, ppmi.T)
    left, right = pl.pallas_call(
        finish_kernel,
        out_shape=[jax.ShapeDtypeStruct((256, rows), BF16), jax.ShapeDtypeStruct((cols, 256), BF16)],
        in_specs=[VMEM] * 3,
        out_specs=[VMEM] * 2,
        scratch_shapes=[pltpu.VMEM((2, 256, 256), F32), pltpu.VMEM((2, 256, 256), F32)],
        compiler_params=pltpu.CompilerParams(vmem_limit_bytes=LIMIT),
    )(gram, y, w)
    return left, right.T


def solution(mesh):
    split = Mesh(mesh.devices.reshape(NY, NZ, NX, NK), ("row", "z", "x", "k"))
    col = ("z", "x", "k")
    return jax.shard_map(
        local,
        mesh=split,
        in_specs=(P("row", col), P(None, col)),
        out_specs=(P(None, "row"), P(None, col)),
        check_vma=False,
    )
```

```python
import functools
import itertools

import jax
import jax.numpy as jnp
from jax import lax
from jax.experimental import pallas as pl
from jax.experimental.pallas import tpu as pltpu
from jax.sharding import Mesh
from jax.sharding import PartitionSpec as P

F32 = jnp.float32
BF16 = jnp.bfloat16
MESH = pl.DeviceIdType.MESH
NY, NZ, NX, NK = 8, 8, 4, 2
SIZES = {"row": NY, "z": NZ, "x": NX, "k": NK}
VMEM = pl.BlockSpec(memory_space=pltpu.VMEM)
LIMIT = 56 << 20


def peer(axis, step):
    return lax.rem(lax.axis_index(axis) + (step + SIZES[axis]), SIZES[axis])


def others(axes):
    steps = [step for step in itertools.product(*(range(SIZES[a]) for a in axes)) if any(step)]
    return sorted(steps, key=lambda step: -sum(min(s, SIZES[a] - s) for s, a in zip(step, axes)))


def greet(*groups):
    barrier = pltpu.get_barrier_semaphore()
    count = 0
    for axes in groups:
        for step in others(axes):
            to = {a: peer(a, s) for a, s in zip(axes, step)}
            pl.semaphore_signal(barrier, inc=1, device_id=to, device_id_type=MESH)
            count += 1
    return lambda: pl.semaphore_wait(barrier, count)


class Exchange:
    def __init__(self, axes, source, target, send, recv):
        self.copies = []
        for step in others(axes):
            to = {a: peer(a, s) for a, s in zip(axes, step)}
            number, slot = 0, 0
            for a, s in zip(axes, step):
                number, slot = number * SIZES[a] + to[a], slot * SIZES[a] + s
            self.copies.append(
                pltpu.make_async_remote_copy(
                    src_ref=source(number),
                    dst_ref=target(slot - 1),
                    send_sem=send.at[slot - 1],
                    recv_sem=recv.at[slot - 1],
                    device_id=to,
                    device_id_type=MESH,
                )
            )
        for copy in self.copies:
            copy.start()

    def arrived(self):
        for copy in self.copies:
            copy.wait_recv()

    def sent(self):
        for copy in self.copies:
            copy.wait_send()


def part(index, size):
    return pl.ds(pl.multiple_of(index * size, size), size)


def tile_of(ref, index, width):
    return ref.at[..., part(index // 2, 8), part(lax.rem(index, 2), width)]


def dot(a, b, dims, precision=None):
    return lax.dot_general(a, b, (dims, ((), ())), precision=precision, preferred_element_type=F32)


def y_kernel(b_ref, p_ref, y_ref, away, home, from_k, from_x, strip, from_z, tile, sends, recvs):
    z, x, k = (lax.axis_index(a) for a in "zxk")
    wait_barrier = greet("z", "x", "k")
    away[...] = dot(p_ref[:, part(1 - k, 256)], b_ref[...], ((0,), (0,)))
    wait_barrier()
    ex = [Exchange("k", lambda to: away, lambda slot: from_k, sends.at[0], recvs.at[0])]
    own = dot(p_ref[:, part(k, 256)], b_ref[...], ((0,), (0,)))
    ex[-1].arrived()
    home[...] = own + from_k[...]
    ex.append(Exchange("x", lambda to: home.at[part(to, 64)], lambda slot: from_x.at[slot], sends.at[1], recvs.at[1]))
    ex[-1].arrived()
    strip[...] = home[part(x, 64), :] + from_x[0] + from_x[1] + from_x[2]
    ex.append(Exchange("z", lambda to: strip.at[part(to, 8)], lambda slot: from_z.at[slot], sends.at[2], recvs.at[2]))
    ex[-1].arrived()
    total = strip[part(z, 8), :]
    for slot in range(NZ - 1):
        total += from_z[slot]
    tile[...] = total
    half = y_ref.at[part(k, 256)]
    rows = half.at[part(x, 64)]
    rows[part(z, 8), :] = total
    ex.append(Exchange("z", lambda to: tile, lambda slot: rows.at[part(z, 8)], sends.at[3], recvs.at[3]))
    ex[-1].arrived()
    ex.append(Exchange("x", lambda to: rows, lambda slot: rows, sends.at[4], recvs.at[4]))
    ex[-1].arrived()
    ex.append(Exchange("k", lambda to: half, lambda slot: half, sends.at[5], recvs.at[5]))
    for e in ex:
        e.sent()
    ex[-1].arrived()


def hop(axis, step, source, target, send, recv):
    copy = pltpu.make_async_remote_copy(
        src_ref=source,
        dst_ref=target,
        send_sem=send,
        recv_sem=recv,
        device_id={axis: peer(axis, step)},
        device_id_type=MESH,
    )
    copy.start()
    return copy


WAYS = (1, -1)


def chain(way, half):
    return 4 if (way == 1) == (half == 0) else 3


SPAN = 250.0


def encode(value, out):
    rows = value.shape[0]
    size = jnp.abs(value).reshape(rows // 8, 8, 256)
    scale = jnp.maximum(jnp.max(size, axis=0) * (1 + 2.0**-7), 1e-30).astype(BF16)
    power = jnp.exp2(size * (SPAN / scale.astype(F32)) - SPAN / 2).reshape(rows, 256)
    out[:rows, :] = jnp.where(value < 0, -power, power).astype(BF16)
    out[rows:, :] = jnp.concatenate([scale, scale], 0)


def decode(coded):
    rows = coded.shape[0] - 16
    value = coded[:rows, :].astype(F32)
    scale = coded[rows : rows + 8, :].astype(F32) * (1 / SPAN)
    size = (jnp.log2(jnp.abs(value)) + SPAN / 2).reshape(rows // 8, 8, 256) * scale
    size = size.reshape(rows, 256)
    return jnp.where(value < 0, -size, size)


class Ring:
    def __init__(self, parts, out, ring, send, recv):
        self.parts, self.out, self.ring, self.send, self.recv = parts, out, ring, send, recv
        self.flight, self.waiting = {}, []

    def step(self, step):
        for half in range(2):
            at = pl.ds(128 * half, 128)
            for w, way in enumerate(WAYS):
                hops = chain(way, half)
                if step >= hops:
                    continue
                total = self.parts[peer("row", way * (hops - step)), at, :]
                if step:
                    self.flight[w, half].wait_recv()
                    total += decode(self.ring[step - 1, w, half])
                encode(total, self.out.at[step, w, half])
                copy = hop(
                    "row",
                    way,
                    self.out.at[step, w, half],
                    self.ring.at[step, w, half],
                    self.send.at[step, w, half],
                    self.recv.at[step, w, half],
                )
                self.waiting.append(copy)
                self.flight[w, half] = copy

    def last(self, target):
        row = lax.axis_index("row")
        for half in range(2):
            at = pl.ds(128 * half, 128)
            total = self.parts[row, at, :]
            for w, way in enumerate(WAYS):
                self.flight[w, half].wait_recv()
                total += decode(self.ring[chain(way, half) - 1, w, half])
            target[at, :] = total


class Gather:
    def __init__(self, blocks, send, recv):
        self.blocks, self.send, self.recv = blocks, send, recv
        self.flight, self.waiting = {}, []

    def step(self, step):
        for half in range(2):
            for w, way in enumerate(WAYS):
                hops = chain(way, half)
                if 0 < step <= hops:
                    self.flight[w, half].wait_recv()
                if step < hops:
                    block = self.blocks.at[peer("row", -way * step), half]
                    copy = hop("row", way, block, block, self.send.at[step, w, half], self.recv.at[step, w, half])
                    self.waiting.append(copy)
                    self.flight[w, half] = copy


def w_kernel(rows_total, cols_total, y_ref, p_ref, g_ref, w_ref, parts, out, ring, mine, gram, gram1, from_k, home, from_zx, tile,
             from_y, piece, rs_send, rs_recv, ag_send, ag_recv, sends, recvs):
    row, k = lax.axis_index("row"), lax.axis_index("k")
    me = lax.axis_index("z") * NX + lax.axis_index("x")
    cols = p_ref.shape[0]
    wait_barrier = greet(("row",), "zx", "k")
    y = y_ref[...]
    high = y.astype(BF16)
    low = (y - high.astype(F32)).astype(BF16)
    for chunk in range(NY):
        width = min(256, cols - 256 * chunk)
        block = p_ref[256 * chunk : 256 * chunk + width, :]
        value = dot(block, high, ((1,), (0,))) + dot(block, low, ((1,), (0,)))
        if width < 256:
            parts[chunk, 128:, :] = jnp.zeros((128, 256), F32)
        parts[chunk, :width, :] = value
    wait_barrier()
    reduce = Ring(parts, out, ring, rs_send, rs_recv)
    for step in range(4):
        reduce.step(step)
    gram1[...] = dot(y, y, ((0,), (0,)), lax.Precision.HIGHEST) / rows_total
    reduce.last(mine)
    for half in range(2):
        encode(mine[pl.ds(128 * half, 128), :], w_ref.at[row, half])
    gram[...] = dot(mine[...], mine[...], ((0,), (0,)), lax.Precision.HIGHEST)
    gather = Gather(w_ref, ag_send, ag_recv)
    ex = [Exchange("k", lambda to: gram.at[part(to, 128)], lambda slot: from_k, sends.at[0], recvs.at[0])]
    gather.step(0)
    ex[-1].arrived()
    home[...] = gram[part(k, 128), :] + from_k[...]
    ex.append(Exchange("zx", lambda to: tile_of(home, to, 128), lambda slot: from_zx.at[slot], sends.at[1], recvs.at[1]))
    gather.step(1)
    ex[-1].arrived()
    total = tile_of(home, me, 128)[...]
    for slot in range(NZ * NX - 1):
        total += from_zx[slot]
    tile[0] = gram1[pl.ds(pl.multiple_of(128 * k + 8 * (me // 2), 8), 8), part(lax.rem(me, 2), 128)]
    tile[1] = total
    from_y[row] = tile[...]
    ex.append(Exchange(("row",), lambda to: tile, lambda slot: from_y.at[row], sends.at[2], recvs.at[2]))
    gather.step(2)
    ex[-1].arrived()
    whole = from_y[0]
    for slot in range(1, NY):
        whole += from_y[slot]
    whole = jnp.stack([whole[0], whole[1] / cols_total])
    piece[...] = whole
    half = g_ref.at[:, part(k, 128)]
    tile_of(half, me, 128)[...] = whole
    ex.append(Exchange("zx", lambda to: piece, lambda slot: tile_of(half, me, 128), sends.at[3], recvs.at[3]))
    gather.step(3)
    ex[-1].arrived()
    ex.append(Exchange("k", lambda to: half, lambda slot: half, sends.at[4], recvs.at[4]))
    gather.step(4)
    for e in ex:
        e.sent()
    ex[-1].arrived()
    for copy in reduce.waiting + gather.waiting:
        copy.wait_send()


def in_three(value):
    high = value.astype(BF16).astype(F32)
    rest = value - high
    middle = rest.astype(BF16).astype(F32)
    return high, middle, rest - middle


def spread_pair(a, b):
    h, m, l = in_three(a)
    i, n, o = in_three(b)
    return jnp.concatenate([h, h, m, h, l, m], 0).astype(BF16), jnp.concatenate([i, n, i, o, i, n], 0).astype(BF16)


def spread(value):
    return jnp.broadcast_to(value, (8, 128))


def eliminate(block, base, count):
    lane = lax.broadcasted_iota(jnp.int32, (8, 128), 1)
    line = lax.broadcasted_iota(jnp.int32, (8, 128), 0)
    groups = count // 8
    tiles = [[block[8 * g : 8 * g + 8, 128 * h : 128 * h + 128] for g in range(groups)] for h in range(2)]
    for now in range(groups):
        side, first = divmod(base + 8 * now, 128)
        rows = [[spread(tiles[h][now][a : a + 1, :]) for h in range(2)] for a in range(8)]
        columns = [
            {g: spread(tiles[side][g][:, first + a : first + a + 1]) for g in range(now, groups)} for a in range(8)
        ]
        corner = {(i, k): spread(columns[k][now][i : i + 1, :]) for i in range(8) for k in range(i + 1)}
        factor, inverse = {}, {}
        for a in range(8):
            root = lax.rsqrt(corner[a, a])
            inverse[a, a] = root
            for i in range(a + 1, 8):
                factor[i, a] = corner[i, a] * root
            for i in range(a + 1, 8):
                for k in range(a + 1, i + 1):
                    corner[i, k] = corner[i, k] - factor[i, a] * factor[k, a]
            for k in range(a):
                total = factor[a, k] * inverse[k, k]
                for q in range(k + 1, a):
                    total = total + factor[a, q] * inverse[q, k]
                inverse[a, k] = -(total * root)
        done = []
        for a in range(8):
            pair = []
            for h in range(2):
                value = inverse[a, 0] * rows[0][h]
                for k in range(1, a + 1):
                    value = value + inverse[a, k] * rows[k][h]
                if h == side:
                    for k in range(8):
                        value = jnp.where(lane == first + k, inverse[a, k] if k <= a else 0.0, value)
                pair.append(value)
            done.append(pair)
        unit = (lane >= first) & (lane < first + 8)
        for g in range(now + 1, groups):
            weights = []
            for a in range(8):
                value = inverse[a, 0] * columns[0][g]
                for k in range(1, a + 1):
                    value = value + inverse[a, k] * columns[k][g]
                weights.append(value)
            for h in range(2):
                change = weights[0] * done[0][h]
                for a in range(1, 8):
                    change = change + weights[a] * done[a][h]
                old = jnp.where(unit, 0.0, tiles[h][g]) if h == side else tiles[h][g]
                tiles[h][g] = old - change
        for h in range(2):
            value = done[0][h]
            for a in range(1, 8):
                value = jnp.where(line == a, done[a][h], value)
            tiles[h][now] = value
    return jnp.concatenate([jnp.concatenate(tiles[h], 0) for h in range(2)], 1)


def finish_kernel(g_ref, y_ref, w_ref, left_ref, right_ref, work, inverse):
    size, count = 256, 16
    work[...] = g_ref[...]
    lane = lax.broadcasted_iota(jnp.int32, (1, size), 1)
    line = lax.broadcasted_iota(jnp.int32, (count, 1), 0)
    for base in range(0, size, count):
        below = base + count
        for q in range(2):
            block = eliminate(work[q, base:below, :], base, count)
            lower = lane <= line + base
            inverse[q, base:below, :] = jnp.where(lower, block, 0.0)
            if below < size:
                a, b = spread_pair(block, jnp.where(lower | (lane >= below), block, 0.0))
                change = dot(a, b, ((0,), (0,)))[below:]
                panel = (lane >= base) & (lane < below)
                work[q, below:, :] = jnp.where(panel, 0.0, work[q, below:, :]) - change
    left_ref[...] = dot(inverse[0], y_ref[...], ((1,), (1,)), lax.Precision.HIGHEST).astype(BF16)
    cols = right_ref.shape[0]
    for chunk in range(2 * NY):
        width = min(128, cols - 128 * chunk)
        value = dot(decode(w_ref[chunk // 2, chunk % 2]), inverse[1], ((1,), (1,)), lax.Precision.HIGHEST)
        right_ref[128 * chunk : 128 * chunk + width, :] = value[:width].astype(BF16)


def local(ppmi, basis):
    rows, cols = ppmi.shape
    rows_total, cols_total = rows * NY, cols * NZ * NX * NK
    dma = pltpu.SemaphoreType.DMA
    params = functools.partial(pltpu.CompilerParams, has_side_effects=True, vmem_limit_bytes=LIMIT)
    y = pl.pallas_call(
        y_kernel,
        out_shape=jax.ShapeDtypeStruct((512, 256), F32),
        in_specs=[VMEM] * 2,
        out_specs=VMEM,
        scratch_shapes=[
            pltpu.VMEM((256, 256), F32),
            pltpu.VMEM((256, 256), F32),
            pltpu.VMEM((256, 256), F32),
            pltpu.VMEM((3, 64, 256), F32),
            pltpu.VMEM((64, 256), F32),
            pltpu.VMEM((7, 8, 256), F32),
            pltpu.VMEM((8, 256), F32),
            dma((6, 7)),
            dma((6, 7)),
        ],
        compiler_params=params(collective_id=0),
    )(basis.T, ppmi.T)
    gram, w = pl.pallas_call(
        functools.partial(w_kernel, rows_total, cols_total),
        out_shape=[jax.ShapeDtypeStruct((2, 256, 256), F32), jax.ShapeDtypeStruct((8, 2, 144, 256), BF16)],
        in_specs=[VMEM] * 2,
        out_specs=[VMEM] * 2,
        scratch_shapes=[
            pltpu.VMEM((8, 256, 256), F32),
            pltpu.VMEM((4, 2, 2, 144, 256), BF16),
            pltpu.VMEM((4, 2, 2, 144, 256), BF16),
            pltpu.VMEM((256, 256), F32),
            pltpu.VMEM((256, 256), F32),
            pltpu.VMEM((256, 256), F32),
            pltpu.VMEM((128, 256), F32),
            pltpu.VMEM((128, 256), F32),
            pltpu.VMEM((31, 8, 128), F32),
            pltpu.VMEM((2, 8, 128), F32),
            pltpu.VMEM((8, 2, 8, 128), F32),
            pltpu.VMEM((2, 8, 128), F32),
            dma((4, 2, 2)),
            dma((4, 2, 2)),
            dma((4, 2, 2)),
            dma((4, 2, 2)),
            dma((5, 31)),
            dma((5, 31)),
        ],
        compiler_params=params(collective_id=1),
    )(y, ppmi.T)
    left, right = pl.pallas_call(
        finish_kernel,
        out_shape=[jax.ShapeDtypeStruct((256, rows), BF16), jax.ShapeDtypeStruct((cols, 256), BF16)],
        in_specs=[VMEM] * 3,
        out_specs=[VMEM] * 2,
        scratch_shapes=[pltpu.VMEM((2, 256, 256), F32), pltpu.VMEM((2, 256, 256), F32)],
        compiler_params=pltpu.CompilerParams(vmem_limit_bytes=LIMIT),
    )(gram, y, w)
    return left, right.T


def solution(mesh):
    split = Mesh(mesh.devices.reshape(NY, NZ, NX, NK), ("row", "z", "x", "k"))
    col = ("z", "x", "k")
    return jax.shard_map(
        local,
        mesh=split,
        in_specs=(P("row", col), P(None, col)),
        out_specs=(P(None, "row"), P(None, col)),
        check_vma=False,
    )
```

```python
import functools
import itertools

import jax
import jax.numpy as jnp
from jax import lax
from jax.experimental import pallas as pl
from jax.experimental.pallas import tpu as pltpu
from jax.sharding import Mesh
from jax.sharding import PartitionSpec as P

F32 = jnp.float32
BF16 = jnp.bfloat16
MESH = pl.DeviceIdType.MESH
NY, NZ, NX, NK = 8, 8, 4, 2
SIZES = {"row": NY, "z": NZ, "x": NX, "k": NK}
VMEM = pl.BlockSpec(memory_space=pltpu.VMEM)
LIMIT = 56 << 20


def peer(axis, step):
    return lax.rem(lax.axis_index(axis) + (step + SIZES[axis]), SIZES[axis])


def others(axes):
    steps = [step for step in itertools.product(*(range(SIZES[a]) for a in axes)) if any(step)]
    return sorted(steps, key=lambda step: -sum(min(s, SIZES[a] - s) for s, a in zip(step, axes)))


def greet(*groups):
    barrier = pltpu.get_barrier_semaphore()
    count = 0
    for axes in groups:
        for step in others(axes):
            to = {a: peer(a, s) for a, s in zip(axes, step)}
            pl.semaphore_signal(barrier, inc=1, device_id=to, device_id_type=MESH)
            count += 1
    return lambda: pl.semaphore_wait(barrier, count)


class Exchange:
    def __init__(self, axes, source, target, send, recv):
        self.copies = []
        for step in others(axes):
            to = {a: peer(a, s) for a, s in zip(axes, step)}
            number, slot = 0, 0
            for a, s in zip(axes, step):
                number, slot = number * SIZES[a] + to[a], slot * SIZES[a] + s
            self.copies.append(
                pltpu.make_async_remote_copy(
                    src_ref=source(number),
                    dst_ref=target(slot - 1),
                    send_sem=send.at[slot - 1],
                    recv_sem=recv.at[slot - 1],
                    device_id=to,
                    device_id_type=MESH,
                )
            )
        for copy in self.copies:
            copy.start()

    def arrived(self):
        for copy in self.copies:
            copy.wait_recv()

    def sent(self):
        for copy in self.copies:
            copy.wait_send()


def part(index, size):
    return pl.ds(pl.multiple_of(index * size, size), size)


def tile_of(ref, index, width):
    return ref.at[..., part(index // 2, 8), part(lax.rem(index, 2), width)]


def dot(a, b, dims, precision=None):
    return lax.dot_general(a, b, (dims, ((), ())), precision=precision, preferred_element_type=F32)


SPAN = 250.0


def encode(value, out):
    rows = value.shape[0]
    size = jnp.abs(value).reshape(rows // 8, 8, 256)
    scale = jnp.maximum(jnp.max(size, axis=0) * (1 + 2.0**-7), 1e-30).astype(BF16)
    power = jnp.exp2(size * (SPAN / scale.astype(F32)) - SPAN / 2).reshape(rows, 256)
    out[:rows, :] = jnp.where(value < 0, -power, power).astype(BF16)
    out[rows:, :] = jnp.concatenate([scale, scale], 0)


def decode(coded):
    rows = coded.shape[0] - 16
    value = coded[:rows, :].astype(F32)
    scale = coded[rows : rows + 8, :].astype(F32) * (1 / SPAN)
    size = (jnp.log2(jnp.abs(value)) + SPAN / 2).reshape(rows // 8, 8, 256) * scale
    size = size.reshape(rows, 256)
    return jnp.where(value < 0, -size, size)


def sum_y(wait_barrier, b_ref, p_ref, y_ref, away, home, from_k, out_x, from_x, strip, from_z, tile, rows, coded, sends, recvs):
    z, x, k = (lax.axis_index(a) for a in "zxk")
    away[...] = dot(p_ref[:, part(1 - k, 256)], b_ref[...], ((0,), (0,)))
    wait_barrier()
    ex = [Exchange("k", lambda to: away, lambda slot: from_k, sends.at[0], recvs.at[0])]
    own = dot(p_ref[:, part(k, 256)], b_ref[...], ((0,), (0,)))
    ex[-1].arrived()
    home[...] = own + from_k[...]
    for number in range(NX):
        encode(home[64 * number : 64 * number + 64, :], out_x.at[number])
    ex.append(Exchange("x", lambda to: out_x.at[to], lambda slot: from_x.at[slot], sends.at[1], recvs.at[1]))
    ex[-1].arrived()
    total = home[part(x, 64), :]
    for slot in range(NX - 1):
        total += decode(from_x[slot])
    strip[...] = total
    ex.append(Exchange("z", lambda to: strip.at[part(to, 8)], lambda slot: from_z.at[slot], sends.at[2], recvs.at[2]))
    ex[-1].arrived()
    total = strip[part(z, 8), :]
    for slot in range(NZ - 1):
        total += from_z[slot]
    tile[...] = total
    rows[part(z, 8), :] = total
    ex.append(Exchange("z", lambda to: tile, lambda slot: rows.at[part(z, 8)], sends.at[3], recvs.at[3]))
    ex[-1].arrived()
    encode(rows[...], coded.at[k, x])
    ex.append(Exchange("x", lambda to: coded.at[k, x], lambda slot: coded.at[k, x], sends.at[4], recvs.at[4]))
    ex[-1].arrived()
    ex.append(Exchange("k", lambda to: coded.at[k], lambda slot: coded.at[k], sends.at[5], recvs.at[5]))
    ex[-1].arrived()
    for number in range(NK * NX):
        y_ref[64 * number : 64 * number + 64, :] = decode(coded[number // NX, number % NX])
    return ex


def hop(axis, step, source, target, send, recv):
    copy = pltpu.make_async_remote_copy(
        src_ref=source,
        dst_ref=target,
        send_sem=send,
        recv_sem=recv,
        device_id={axis: peer(axis, step)},
        device_id_type=MESH,
    )
    copy.start()
    return copy


WAYS = (1, -1)


def chain(way, half):
    return 4 if (way == 1) == (half == 0) else 3


class Ring:
    def __init__(self, parts, out, ring, send, recv):
        self.parts, self.out, self.ring, self.send, self.recv = parts, out, ring, send, recv
        self.flight, self.waiting = {}, []

    def step(self, step):
        for half in range(2):
            at = pl.ds(128 * half, 128)
            for w, way in enumerate(WAYS):
                hops = chain(way, half)
                if step >= hops:
                    continue
                total = self.parts[peer("row", way * (hops - step)), at, :]
                if step:
                    self.flight[w, half].wait_recv()
                    total += decode(self.ring[step - 1, w, half])
                encode(total, self.out.at[step, w, half])
                copy = hop(
                    "row",
                    way,
                    self.out.at[step, w, half],
                    self.ring.at[step, w, half],
                    self.send.at[step, w, half],
                    self.recv.at[step, w, half],
                )
                self.waiting.append(copy)
                self.flight[w, half] = copy

    def last(self, target):
        row = lax.axis_index("row")
        for half in range(2):
            at = pl.ds(128 * half, 128)
            total = self.parts[row, at, :]
            for w, way in enumerate(WAYS):
                self.flight[w, half].wait_recv()
                total += decode(self.ring[chain(way, half) - 1, w, half])
            target[at, :] = total


class Gather:
    def __init__(self, blocks, send, recv):
        self.blocks, self.send, self.recv = blocks, send, recv
        self.flight, self.waiting = {}, []

    def step(self, step):
        for half in range(2):
            for w, way in enumerate(WAYS):
                hops = chain(way, half)
                if 0 < step <= hops:
                    self.flight[w, half].wait_recv()
                if step < hops:
                    block = self.blocks.at[peer("row", -way * step), half]
                    copy = hop("row", way, block, block, self.send.at[step, w, half], self.recv.at[step, w, half])
                    self.waiting.append(copy)
                    self.flight[w, half] = copy


def in_three(value):
    high = value.astype(BF16).astype(F32)
    rest = value - high
    middle = rest.astype(BF16).astype(F32)
    return high, middle, rest - middle


def spread_pair(a, b):
    h, m, l = in_three(a)
    i, n, o = in_three(b)
    return jnp.concatenate([h, h, m, h, l, m], 0).astype(BF16), jnp.concatenate([i, n, i, o, i, n], 0).astype(BF16)


def spread(value):
    return jnp.broadcast_to(value, (8, 128))


def eliminate(block, base, count):
    lane = lax.broadcasted_iota(jnp.int32, (8, 128), 1)
    line = lax.broadcasted_iota(jnp.int32, (8, 128), 0)
    groups = count // 8
    tiles = [[block[8 * g : 8 * g + 8, 128 * h : 128 * h + 128] for g in range(groups)] for h in range(2)]
    for now in range(groups):
        side, first = divmod(base + 8 * now, 128)
        rows = [[spread(tiles[h][now][a : a + 1, :]) for h in range(2)] for a in range(8)]
        columns = [
            {g: spread(tiles[side][g][:, first + a : first + a + 1]) for g in range(now, groups)} for a in range(8)
        ]
        corner = {(i, k): spread(columns[k][now][i : i + 1, :]) for i in range(8) for k in range(i + 1)}
        factor, inverse = {}, {}
        for a in range(8):
            root = lax.rsqrt(corner[a, a])
            inverse[a, a] = root
            for i in range(a + 1, 8):
                factor[i, a] = corner[i, a] * root
            for i in range(a + 1, 8):
                for k in range(a + 1, i + 1):
                    corner[i, k] = corner[i, k] - factor[i, a] * factor[k, a]
            for k in range(a):
                total = factor[a, k] * inverse[k, k]
                for q in range(k + 1, a):
                    total = total + factor[a, q] * inverse[q, k]
                inverse[a, k] = -(total * root)
        done = []
        for a in range(8):
            pair = []
            for h in range(2):
                value = inverse[a, 0] * rows[0][h]
                for k in range(1, a + 1):
                    value = value + inverse[a, k] * rows[k][h]
                if h == side:
                    for k in range(8):
                        value = jnp.where(lane == first + k, inverse[a, k] if k <= a else 0.0, value)
                pair.append(value)
            done.append(pair)
        unit = (lane >= first) & (lane < first + 8)
        for g in range(now + 1, groups):
            weights = []
            for a in range(8):
                value = inverse[a, 0] * columns[0][g]
                for k in range(1, a + 1):
                    value = value + inverse[a, k] * columns[k][g]
                weights.append(value)
            for h in range(2):
                change = weights[0] * done[0][h]
                for a in range(1, 8):
                    change = change + weights[a] * done[a][h]
                old = jnp.where(unit, 0.0, tiles[h][g]) if h == side else tiles[h][g]
                tiles[h][g] = old - change
        for h in range(2):
            value = done[0][h]
            for a in range(1, 8):
                value = jnp.where(line == a, done[a][h], value)
            tiles[h][now] = value
    return jnp.concatenate([jnp.concatenate(tiles[h], 0) for h in range(2)], 1)


def inverse_steps(work, inverse):
    size, count = 256, 16
    lane = lax.broadcasted_iota(jnp.int32, (1, size), 1)
    line = lax.broadcasted_iota(jnp.int32, (count, 1), 0)
    for base in range(0, size, count):
        below = base + count
        block = eliminate(work[base:below, :], base, count)
        lower = lane <= line + base
        inverse[base:below, :] = jnp.where(lower, block, 0.0)
        if below < size:
            a, b = spread_pair(block, jnp.where(lower | (lane >= below), block, 0.0))
            change = dot(a, b, ((0,), (0,)))[below:]
            panel = (lane >= base) & (lane < below)
            work[below:, :] = jnp.where(panel, 0.0, work[below:, :]) - change
        yield


def take(steps, count):
    for _ in range(count):
        next(steps, None)


def sum_kernel(rows_total, cols_total, b_ref, p_ref, left_ref, g_ref, w_ref, away, y_home, y_from_k, out_x, from_x, strip, from_z,
               y_tile, y_rows, coded, y_ref, parts, out, ring, mine, gram, gram1, total1, from_k, home, from_zx, tile, from_y, piece, inverse,
               y_sends, y_recvs, rs_send, rs_recv, ag_send, ag_recv, sends, recvs):
    row, k = lax.axis_index("row"), lax.axis_index("k")
    me = lax.axis_index("z") * NX + lax.axis_index("x")
    cols = p_ref.shape[0]
    wait_barrier = greet(("row",), "zx", "k")
    ex = sum_y(wait_barrier, b_ref, p_ref, y_ref, away, y_home, y_from_k, out_x, from_x, strip, from_z, y_tile, y_rows, coded,
               y_sends, y_recvs)
    y = y_ref[...]
    high = y.astype(BF16)
    low = (y - high.astype(F32)).astype(BF16)
    for chunk in range(NY):
        width = min(256, cols - 256 * chunk)
        block = p_ref[256 * chunk : 256 * chunk + width, :]
        value = dot(block, high, ((1,), (0,))) + dot(block, low, ((1,), (0,)))
        if width < 256:
            parts[chunk, 128:, :] = jnp.zeros((128, 256), F32)
        parts[chunk, :width, :] = value
    reduce = Ring(parts, out, ring, rs_send, rs_recv)
    reduce.step(0)

    def exchange(axes, source, target):
        number = len(ex) - 6
        ex.append(Exchange(axes, source, target, sends.at[number], recvs.at[number]))

    def over_rows(which):
        ex[-1].arrived()
        whole = from_y[which, 0]
        for number in range(1, NY):
            whole += from_y[which, number]
        return whole

    gram1[...] = dot(y, y, ((0,), (0,)), lax.Precision.HIGHEST) / rows_total
    own = gram1[pl.ds(pl.multiple_of(128 * k + 8 * (me // 2), 8), 8), part(lax.rem(me, 2), 128)]
    tile[0] = own
    from_y[0, row] = own
    exchange(("row",), lambda to: tile.at[0], lambda slot: from_y.at[0, row])
    reduce.step(1)
    whole = over_rows(0)
    piece[0] = whole
    half1 = total1.at[part(k, 128)]
    tile_of(half1, me, 128)[...] = whole
    exchange("zx", lambda to: piece.at[0], lambda slot: tile_of(half1, me, 128))
    reduce.step(2)
    ex[-1].arrived()
    exchange("k", lambda to: half1, lambda slot: half1)
    reduce.step(3)
    ex[-1].arrived()
    gram1[...] = total1[...]
    steps = inverse_steps(gram1, inverse)
    take(steps, 1)
    reduce.last(mine)
    gram[...] = dot(mine[...], mine[...], ((0,), (0,)), lax.Precision.HIGHEST)
    gather = Gather(w_ref, ag_send, ag_recv)
    exchange("k", lambda to: gram.at[part(to, 128)], lambda slot: from_k)
    for half in range(2):
        encode(mine[pl.ds(128 * half, 128), :], w_ref.at[row, half])
    gather.step(0)
    take(steps, 2)
    ex[-1].arrived()
    home[...] = gram[part(k, 128), :] + from_k[...]
    exchange("zx", lambda to: tile_of(home, to, 128), lambda slot: from_zx.at[slot])
    take(steps, 3)
    gather.step(1)
    take(steps, 3)
    ex[-1].arrived()
    total = tile_of(home, me, 128)[...]
    for slot in range(NZ * NX - 1):
        total += from_zx[slot]
    tile[1] = total
    from_y[1, row] = total
    exchange(("row",), lambda to: tile.at[1], lambda slot: from_y.at[1, row])
    gather.step(2)
    take(steps, 5)
    whole = over_rows(1) / cols_total
    piece[1] = whole
    half2 = g_ref.at[part(k, 128)]
    tile_of(half2, me, 128)[...] = whole
    exchange("zx", lambda to: piece.at[1], lambda slot: tile_of(half2, me, 128))
    gather.step(3)
    take(steps, 16)
    left_ref[...] = dot(inverse[...], y_ref[...], ((1,), (1,)), lax.Precision.HIGHEST).astype(BF16)
    ex[-1].arrived()
    exchange("k", lambda to: half2, lambda slot: half2)
    gather.step(4)
    for e in ex:
        e.sent()
    ex[-1].arrived()
    for copy in reduce.waiting + gather.waiting:
        copy.wait_send()


def halves(value):
    high = value.astype(BF16)
    return high, (value - high.astype(F32)).astype(BF16)


def finish_kernel(g_ref, w_ref, before_ref, right_ref, left_ref, work, inverse, wide):
    left_ref[...] = before_ref[...]
    work[...] = g_ref[...]
    for chunk, _ in enumerate(inverse_steps(work, inverse)):
        high, low = halves(decode(w_ref[chunk // 2, chunk % 2]))
        wide[chunk] = jnp.concatenate([high, high, low], 1)
    high, low = halves(inverse[...])
    factor = jnp.concatenate([high, low, high], 1)
    cols = right_ref.shape[0]
    for chunk in range(2 * NY):
        width = min(128, cols - 128 * chunk)
        value = dot(wide[chunk], factor, ((1,), (1,)))
        right_ref[128 * chunk : 128 * chunk + width, :] = value[:width].astype(BF16)


def local(ppmi, basis):
    rows, cols = ppmi.shape
    rows_total, cols_total = rows * NY, cols * NZ * NX * NK
    dma = pltpu.SemaphoreType.DMA
    vmem = pltpu.VMEM
    left, gram, w = pl.pallas_call(
        functools.partial(sum_kernel, rows_total, cols_total),
        out_shape=[
            jax.ShapeDtypeStruct((256, rows), BF16),
            jax.ShapeDtypeStruct((256, 256), F32),
            jax.ShapeDtypeStruct((8, 2, 144, 256), BF16),
        ],
        in_specs=[VMEM] * 2,
        out_specs=[VMEM] * 3,
        scratch_shapes=[
            vmem((256, 256), F32),
            vmem((256, 256), F32),
            vmem((256, 256), F32),
            vmem((4, 80, 256), BF16),
            vmem((3, 80, 256), BF16),
            vmem((64, 256), F32),
            vmem((7, 8, 256), F32),
            vmem((8, 256), F32),
            vmem((64, 256), F32),
            vmem((2, 4, 80, 256), BF16),
            vmem((512, 256), F32),
            vmem((8, 256, 256), F32),
            vmem((4, 2, 2, 144, 256), BF16),
            vmem((4, 2, 2, 144, 256), BF16),
            vmem((256, 256), F32),
            vmem((256, 256), F32),
            vmem((256, 256), F32),
            vmem((256, 256), F32),
            vmem((128, 256), F32),
            vmem((128, 256), F32),
            vmem((31, 8, 128), F32),
            vmem((2, 8, 128), F32),
            vmem((2, 8, 8, 128), F32),
            vmem((2, 8, 128), F32),
            vmem((256, 256), F32),
            dma((6, 7)),
            dma((6, 7)),
            dma((4, 2, 2)),
            dma((4, 2, 2)),
            dma((4, 2, 2)),
            dma((4, 2, 2)),
            dma((8, 31)),
            dma((8, 31)),
        ],
        compiler_params=pltpu.CompilerParams(collective_id=0, has_side_effects=True, vmem_limit_bytes=LIMIT),
    )(basis.T, ppmi.T)
    right, left = pl.pallas_call(
        finish_kernel,
        out_shape=[jax.ShapeDtypeStruct((cols, 256), BF16), jax.ShapeDtypeStruct((256, rows), BF16)],
        in_specs=[VMEM] * 3,
        out_specs=[VMEM] * 2,
        scratch_shapes=[vmem((256, 256), F32), vmem((256, 256), F32), vmem((16, 128, 768), BF16)],
        compiler_params=pltpu.CompilerParams(vmem_limit_bytes=LIMIT),
    )(gram, w, left)
    return left, right.T


def solution(mesh):
    split = Mesh(mesh.devices.reshape(NY, NZ, NX, NK), ("row", "z", "x", "k"))
    col = ("z", "x", "k")
    return jax.shard_map(
        local,
        mesh=split,
        in_specs=(P("row", col), P(None, col)),
        out_specs=(P(None, "row"), P(None, col)),
        check_vma=False,
    )
```

```python
import functools
import itertools

import jax
import jax.numpy as jnp
from jax import lax
from jax.experimental import pallas as pl
from jax.experimental.pallas import tpu as pltpu
from jax.sharding import Mesh
from jax.sharding import PartitionSpec as P

F32 = jnp.float32
BF16 = jnp.bfloat16
MESH = pl.DeviceIdType.MESH
NY, NZ, NX, NK = 8, 8, 4, 2
SIZES = {"row": NY, "z": NZ, "x": NX, "k": NK}
VMEM = pl.BlockSpec(memory_space=pltpu.VMEM)
LIMIT = 56 << 20
COUNT = 32
LATE = 1
CUT = 1


def peer(axis, step):
    return lax.rem(lax.axis_index(axis) + (step + SIZES[axis]), SIZES[axis])


def others(axes):
    steps = [step for step in itertools.product(*(range(SIZES[a]) for a in axes)) if any(step)]
    return sorted(steps, key=lambda step: -sum(min(s, SIZES[a] - s) for s, a in zip(step, axes)))


def greet(*groups):
    barrier = pltpu.get_barrier_semaphore()
    count = 0
    for axes in groups:
        for step in others(axes):
            to = {a: peer(a, s) for a, s in zip(axes, step)}
            pl.semaphore_signal(barrier, inc=1, device_id=to, device_id_type=MESH)
            count += 1
    return lambda: pl.semaphore_wait(barrier, count)


class Exchange:
    def __init__(self, axes, source, target, send, recv):
        self.copies = []
        for step in others(axes):
            to = {a: peer(a, s) for a, s in zip(axes, step)}
            number, slot = 0, 0
            for a, s in zip(axes, step):
                number, slot = number * SIZES[a] + to[a], slot * SIZES[a] + s
            self.copies.append(
                pltpu.make_async_remote_copy(
                    src_ref=source(number),
                    dst_ref=target(slot - 1),
                    send_sem=send.at[slot - 1],
                    recv_sem=recv.at[slot - 1],
                    device_id=to,
                    device_id_type=MESH,
                )
            )
        for copy in self.copies:
            copy.start()

    def arrived(self):
        for copy in self.copies:
            copy.wait_recv()

    def sent(self):
        for copy in self.copies:
            copy.wait_send()


def part(index, size):
    return pl.ds(pl.multiple_of(index * size, size), size)


def tile_of(ref, index, width):
    return ref.at[..., part(index // 2, 8), part(lax.rem(index, 2), width)]


def dot(a, b, dims, precision=None):
    return lax.dot_general(a, b, (dims, ((), ())), precision=precision, preferred_element_type=F32)


SPAN = 250.0


def encode(value, out):
    rows = value.shape[0]
    size = jnp.abs(value).reshape(rows // 8, 8, 256)
    scale = jnp.maximum(jnp.max(size, axis=0) * (1 + 2.0**-7), 1e-30).astype(BF16)
    power = jnp.exp2(size * (SPAN / scale.astype(F32)) - SPAN / 2).reshape(rows, 256)
    out[:rows, :] = jnp.where(value < 0, -power, power).astype(BF16)
    out[rows:, :] = jnp.concatenate([scale, scale], 0)


def decode(coded):
    rows = coded.shape[0] - 16
    value = coded[:rows, :].astype(F32)
    scale = coded[rows : rows + 8, :].astype(F32) * (1 / SPAN)
    size = (jnp.log2(jnp.abs(value)) + SPAN / 2).reshape(rows // 8, 8, 256) * scale
    size = size.reshape(rows, 256)
    return jnp.where(value < 0, -size, size)


def sum_y(wait_barrier, b_ref, p_ref, y_ref, away, home, from_k, out_x, from_x, strip, from_z, tile, rows, coded, sends, recvs):
    z, x, k = (lax.axis_index(a) for a in "zxk")
    away[...] = dot(p_ref[:, part(1 - k, 256)], b_ref[...], ((0,), (0,)))
    wait_barrier()
    ex = [Exchange("k", lambda to: away, lambda slot: from_k, sends.at[0], recvs.at[0])]
    own = dot(p_ref[:, part(k, 256)], b_ref[...], ((0,), (0,)))
    ex[-1].arrived()
    home[...] = own + from_k[...]
    for number in range(NX):
        encode(home[64 * number : 64 * number + 64, :], out_x.at[number])
    ex.append(Exchange("x", lambda to: out_x.at[to], lambda slot: from_x.at[slot], sends.at[1], recvs.at[1]))
    ex[-1].arrived()
    total = home[part(x, 64), :]
    for slot in range(NX - 1):
        total += decode(from_x[slot])
    strip[...] = total
    ex.append(Exchange("z", lambda to: strip.at[part(to, 8)], lambda slot: from_z.at[slot], sends.at[2], recvs.at[2]))
    ex[-1].arrived()
    total = strip[part(z, 8), :]
    for slot in range(NZ - 1):
        total += from_z[slot]
    tile[...] = total
    rows[part(z, 8), :] = total
    ex.append(Exchange("z", lambda to: tile, lambda slot: rows.at[part(z, 8)], sends.at[3], recvs.at[3]))
    ex[-1].arrived()
    encode(rows[...], coded.at[k, x])
    ex.append(Exchange("x", lambda to: coded.at[k, x], lambda slot: coded.at[k, x], sends.at[4], recvs.at[4]))
    ex[-1].arrived()
    ex.append(Exchange("k", lambda to: coded.at[k], lambda slot: coded.at[k], sends.at[5], recvs.at[5]))
    ex[-1].arrived()
    for number in range(NK * NX):
        y_ref[64 * number : 64 * number + 64, :] = decode(coded[number // NX, number % NX])
    return ex


def hop(axis, step, source, target, send, recv):
    copy = pltpu.make_async_remote_copy(
        src_ref=source,
        dst_ref=target,
        send_sem=send,
        recv_sem=recv,
        device_id={axis: peer(axis, step)},
        device_id_type=MESH,
    )
    copy.start()
    return copy


WAYS = (1, -1)


def chain(way, half):
    return 4 if (way == 1) == (half == 0) else 3


class Ring:
    def __init__(self, parts, out, ring, send, recv):
        self.parts, self.out, self.ring, self.send, self.recv = parts, out, ring, send, recv
        self.flight, self.waiting = {}, []

    def step(self, step):
        for half in range(2):
            at = pl.ds(128 * half, 128)
            for w, way in enumerate(WAYS):
                hops = chain(way, half)
                if step >= hops:
                    continue
                total = self.parts[peer("row", way * (hops - step)), at, :]
                if step:
                    self.flight[w, half].wait_recv()
                    total += decode(self.ring[step - 1, w, half])
                encode(total, self.out.at[step, w, half])
                copy = hop(
                    "row",
                    way,
                    self.out.at[step, w, half],
                    self.ring.at[step, w, half],
                    self.send.at[step, w, half],
                    self.recv.at[step, w, half],
                )
                self.waiting.append(copy)
                self.flight[w, half] = copy

    def last(self, target):
        row = lax.axis_index("row")
        for half in range(2):
            at = pl.ds(128 * half, 128)
            total = self.parts[row, at, :]
            for w, way in enumerate(WAYS):
                self.flight[w, half].wait_recv()
                total += decode(self.ring[chain(way, half) - 1, w, half])
            target[at, :] = total


class Gather:
    def __init__(self, blocks, send, recv):
        self.blocks, self.send, self.recv = blocks, send, recv
        self.flight, self.waiting = {}, []

    def step(self, step):
        for half in range(2):
            for w, way in enumerate(WAYS):
                hops = chain(way, half)
                if 0 < step <= hops:
                    self.flight[w, half].wait_recv()
                if step < hops:
                    block = self.blocks.at[peer("row", -way * step), half]
                    copy = hop("row", way, block, block, self.send.at[step, w, half], self.recv.at[step, w, half])
                    self.waiting.append(copy)
                    self.flight[w, half] = copy


def in_three(value):
    high = value.astype(BF16).astype(F32)
    rest = value - high
    middle = rest.astype(BF16).astype(F32)
    return high, middle, rest - middle


def spread_pair(a, b):
    h, m, l = in_three(a)
    i, n, o = in_three(b)
    return jnp.concatenate([h, h, m, h, l, m], 0).astype(BF16), jnp.concatenate([i, n, i, o, i, n], 0).astype(BF16)


def spread(value):
    return jnp.broadcast_to(value, (8, 128))


def eliminate(block, base, count):
    lane = lax.broadcasted_iota(jnp.int32, (8, 128), 1)
    line = lax.broadcasted_iota(jnp.int32, (8, 128), 0)
    groups = count // 8
    tiles = [[block[8 * g : 8 * g + 8, 128 * h : 128 * h + 128] for g in range(groups)] for h in range(2)]
    for now in range(groups):
        side, first = divmod(base + 8 * now, 128)
        rows = [[spread(tiles[h][now][a : a + 1, :]) for h in range(2)] for a in range(8)]
        columns = [
            {g: spread(tiles[side][g][:, first + a : first + a + 1]) for g in range(now, groups)} for a in range(8)
        ]
        corner = {(i, k): spread(columns[k][now][i : i + 1, :]) for i in range(8) for k in range(i + 1)}
        factor, inverse = {}, {}
        for a in range(8):
            root = lax.rsqrt(corner[a, a])
            inverse[a, a] = root
            for i in range(a + 1, 8):
                factor[i, a] = corner[i, a] * root
            for i in range(a + 1, 8):
                for k in range(a + 1, i + 1):
                    corner[i, k] = corner[i, k] - factor[i, a] * factor[k, a]
            for k in range(a):
                total = factor[a, k] * inverse[k, k]
                for q in range(k + 1, a):
                    total = total + factor[a, q] * inverse[q, k]
                inverse[a, k] = -(total * root)
        done = []
        for a in range(8):
            pair = []
            for h in range(2):
                value = inverse[a, 0] * rows[0][h]
                for k in range(1, a + 1):
                    value = value + inverse[a, k] * rows[k][h]
                if h == side:
                    for k in range(8):
                        value = jnp.where(lane == first + k, inverse[a, k] if k <= a else 0.0, value)
                pair.append(value)
            done.append(pair)
        unit = (lane >= first) & (lane < first + 8)
        for g in range(now + 1, groups):
            weights = []
            for a in range(8):
                value = inverse[a, 0] * columns[0][g]
                for k in range(1, a + 1):
                    value = value + inverse[a, k] * columns[k][g]
                weights.append(value)
            for h in range(2):
                change = weights[0] * done[0][h]
                for a in range(1, 8):
                    change = change + weights[a] * done[a][h]
                old = jnp.where(unit, 0.0, tiles[h][g]) if h == side else tiles[h][g]
                tiles[h][g] = old - change
        for h in range(2):
            value = done[0][h]
            for a in range(1, 8):
                value = jnp.where(line == a, done[a][h], value)
            tiles[h][now] = value
    return jnp.concatenate([jnp.concatenate(tiles[h], 0) for h in range(2)], 1)


def inverse_steps(work, inverse, count=16):
    size = 256
    lane = lax.broadcasted_iota(jnp.int32, (1, size), 1)
    line = lax.broadcasted_iota(jnp.int32, (count, 1), 0)
    for base in range(0, size, count):
        below = base + count
        block = eliminate(work[base:below, :], base, count)
        lower = lane <= line + base
        inverse[base:below, :] = jnp.where(lower, block, 0.0)
        if below < size:
            a, b = spread_pair(block, jnp.where(lower | (lane >= below), block, 0.0))
            skip = below // 128 * 128 if CUT else 0
            change = dot(a[:, skip:], b, ((0,), (0,)))[below - skip :]
            panel = (lane >= base) & (lane < below)
            work[below:, :] = jnp.where(panel, 0.0, work[below:, :]) - change
        yield


def take(steps, count):
    for _ in range(count):
        next(steps, None)


def sum_kernel(rows_total, cols_total, b_ref, p_ref, left_ref, g_ref, w_ref, away, y_home, y_from_k, out_x, from_x, strip, from_z,
               y_tile, y_rows, coded, y_ref, parts, out, ring, mine, gram, gram1, total1, from_k, home, from_zx, tile, from_y, piece, inverse,
               y_sends, y_recvs, rs_send, rs_recv, ag_send, ag_recv, sends, recvs):
    row, k = lax.axis_index("row"), lax.axis_index("k")
    me = lax.axis_index("z") * NX + lax.axis_index("x")
    cols = p_ref.shape[0]
    wait_barrier = greet(("row",), "zx", "k")
    ex = sum_y(wait_barrier, b_ref, p_ref, y_ref, away, y_home, y_from_k, out_x, from_x, strip, from_z, y_tile, y_rows, coded,
               y_sends, y_recvs)
    y = y_ref[...]
    high = y.astype(BF16)
    low = (y - high.astype(F32)).astype(BF16)
    for chunk in range(NY):
        width = min(256, cols - 256 * chunk)
        block = p_ref[256 * chunk : 256 * chunk + width, :]
        value = dot(block, high, ((1,), (0,))) + dot(block, low, ((1,), (0,)))
        if width < 256:
            parts[chunk, 128:, :] = jnp.zeros((128, 256), F32)
        parts[chunk, :width, :] = value
    reduce = Ring(parts, out, ring, rs_send, rs_recv)
    reduce.step(0)

    def exchange(axes, source, target):
        number = len(ex) - 6
        ex.append(Exchange(axes, source, target, sends.at[number], recvs.at[number]))

    def over_rows(which):
        ex[-1].arrived()
        whole = from_y[which, 0]
        for number in range(1, NY):
            whole += from_y[which, number]
        return whole

    gram1[...] = dot(y, y, ((0,), (0,)), lax.Precision.HIGHEST) / rows_total
    own = gram1[pl.ds(pl.multiple_of(128 * k + 8 * (me // 2), 8), 8), part(lax.rem(me, 2), 128)]
    tile[0] = own
    from_y[0, row] = own
    exchange(("row",), lambda to: tile.at[0], lambda slot: from_y.at[0, row])
    reduce.step(1)
    whole = over_rows(0)
    piece[0] = whole
    half1 = total1.at[part(k, 128)]
    tile_of(half1, me, 128)[...] = whole
    exchange("zx", lambda to: piece.at[0], lambda slot: tile_of(half1, me, 128))
    reduce.step(2)
    ex[-1].arrived()
    exchange("k", lambda to: half1, lambda slot: half1)
    reduce.step(3)
    ex[-1].arrived()
    gram1[...] = total1[...]
    steps = inverse_steps(gram1, inverse)
    take(steps, 1)
    reduce.last(mine)
    gram[...] = dot(mine[...], mine[...], ((0,), (0,)), lax.Precision.HIGHEST)
    gather = Gather(w_ref, ag_send, ag_recv)
    exchange("k", lambda to: gram.at[part(to, 128)], lambda slot: from_k)
    for half in range(2):
        encode(mine[pl.ds(128 * half, 128), :], w_ref.at[row, half])
    gather.step(0)
    take(steps, 2)
    ex[-1].arrived()
    home[...] = gram[part(k, 128), :] + from_k[...]
    exchange("zx", lambda to: tile_of(home, to, 128), lambda slot: from_zx.at[slot])
    take(steps, 3)
    gather.step(1)
    take(steps, 3)
    ex[-1].arrived()
    total = tile_of(home, me, 128)[...]
    for slot in range(NZ * NX - 1):
        total += from_zx[slot]
    tile[1] = total
    from_y[1, row] = total
    exchange(("row",), lambda to: tile.at[1], lambda slot: from_y.at[1, row])
    if not LATE:
        gather.step(2)
    take(steps, 5)
    whole = over_rows(1) / cols_total
    piece[1] = whole
    half2 = g_ref.at[part(k, 128)]
    tile_of(half2, me, 128)[...] = whole
    exchange("zx", lambda to: piece.at[1], lambda slot: tile_of(half2, me, 128))
    if LATE:
        gather.step(2)
        take(steps, 2)
    gather.step(3)
    take(steps, 16)
    left_ref[...] = dot(inverse[...], y_ref[...], ((1,), (1,)), lax.Precision.HIGHEST).astype(BF16)
    ex[-1].arrived()
    exchange("k", lambda to: half2, lambda slot: half2)
    gather.step(4)
    for e in ex:
        e.sent()
    ex[-1].arrived()
    for copy in reduce.waiting + gather.waiting:
        copy.wait_send()


def halves(value):
    high = value.astype(BF16)
    return high, (value - high.astype(F32)).astype(BF16)


def finish_kernel(g_ref, w_ref, before_ref, right_ref, left_ref, work, inverse, wide):
    left_ref[...] = before_ref[...]
    work[...] = g_ref[...]
    for number, _ in enumerate(inverse_steps(work, inverse, COUNT)):
        for chunk in range(number * COUNT // 16, (number + 1) * COUNT // 16):
            high, low = halves(decode(w_ref[chunk // 2, chunk % 2]))
            wide[chunk] = jnp.concatenate([high, high, low], 1)
    high, low = halves(inverse[...])
    factor = jnp.concatenate([high, low, high], 1)
    cols = right_ref.shape[0]
    for chunk in range(2 * NY):
        width = min(128, cols - 128 * chunk)
        value = dot(wide[chunk], factor, ((1,), (1,)))
        right_ref[128 * chunk : 128 * chunk + width, :] = value[:width].astype(BF16)


def local(ppmi, basis):
    rows, cols = ppmi.shape
    rows_total, cols_total = rows * NY, cols * NZ * NX * NK
    dma = pltpu.SemaphoreType.DMA
    vmem = pltpu.VMEM
    left, gram, w = pl.pallas_call(
        functools.partial(sum_kernel, rows_total, cols_total),
        out_shape=[
            jax.ShapeDtypeStruct((256, rows), BF16),
            jax.ShapeDtypeStruct((256, 256), F32),
            jax.ShapeDtypeStruct((8, 2, 144, 256), BF16),
        ],
        in_specs=[VMEM] * 2,
        out_specs=[VMEM] * 3,
        scratch_shapes=[
            vmem((256, 256), F32),
            vmem((256, 256), F32),
            vmem((256, 256), F32),
            vmem((4, 80, 256), BF16),
            vmem((3, 80, 256), BF16),
            vmem((64, 256), F32),
            vmem((7, 8, 256), F32),
            vmem((8, 256), F32),
            vmem((64, 256), F32),
            vmem((2, 4, 80, 256), BF16),
            vmem((512, 256), F32),
            vmem((8, 256, 256), F32),
            vmem((4, 2, 2, 144, 256), BF16),
            vmem((4, 2, 2, 144, 256), BF16),
            vmem((256, 256), F32),
            vmem((256, 256), F32),
            vmem((256, 256), F32),
            vmem((256, 256), F32),
            vmem((128, 256), F32),
            vmem((128, 256), F32),
            vmem((31, 8, 128), F32),
            vmem((2, 8, 128), F32),
            vmem((2, 8, 8, 128), F32),
            vmem((2, 8, 128), F32),
            vmem((256, 256), F32),
            dma((6, 7)),
            dma((6, 7)),
            dma((4, 2, 2)),
            dma((4, 2, 2)),
            dma((4, 2, 2)),
            dma((4, 2, 2)),
            dma((8, 31)),
            dma((8, 31)),
        ],
        compiler_params=pltpu.CompilerParams(collective_id=0, has_side_effects=True, vmem_limit_bytes=LIMIT),
    )(basis.T, ppmi.T)
    right, left = pl.pallas_call(
        finish_kernel,
        out_shape=[jax.ShapeDtypeStruct((cols, 256), BF16), jax.ShapeDtypeStruct((256, rows), BF16)],
        in_specs=[VMEM] * 3,
        out_specs=[VMEM] * 2,
        scratch_shapes=[vmem((256, 256), F32), vmem((256, 256), F32), vmem((16, 128, 768), BF16)],
        compiler_params=pltpu.CompilerParams(vmem_limit_bytes=LIMIT),
    )(gram, w, left)
    return left, right.T


def solution(mesh):
    split = Mesh(mesh.devices.reshape(NY, NZ, NX, NK), ("row", "z", "x", "k"))
    col = ("z", "x", "k")
    return jax.shard_map(
        local,
        mesh=split,
        in_specs=(P("row", col), P(None, col)),
        out_specs=(P(None, "row"), P(None, col)),
        check_vma=False,
    )
```
